32 devices in a mesh: front: 1, row: 16 (over z, y, x), col: 2 (over core).
Axes of the slice: x: 2, y: 2, z: 4, core: 2. Of those that a mesh axis runs over, the one named last changes fastest.
Arguments:
- contributions: float32 [16, 128, 4096], P(('front', 'row'), None, 'col'), may hold values from -0.176776695 to 0.176776695
- valid_rows: int32 [16], P(('front', 'row')), may hold values from 1 to 128, 1280 in all
Outputs:
- r_rows: float32 [512, 4096], P('front', 'col')
The draws below stay inside these ranges and needn't reach their ends.
All inputs are finite; a program needn't handle non-finite values. No bound on the sum of `valid_rows` on one device may be relied on, other than what follows from the above.
Results may differ from the reference program's by a relative error of at most 0.0003.
Values sent between devices are 32-bit elements; how exact they have to be, the bound alone decides.
A program may use at most 64 MiB of HBM per device.

```python
import math
import jax
import jax.numpy as jnp
import numpy as np
from jax import lax

W = 4096
PANEL = 256
NPANEL = 2
BLOCK = 128
NBLK = 16


def draw_contributions(key, part):
    full_shape = (NBLK, BLOCK, W)
    spread = 1.0 / math.sqrt(BLOCK * NBLK)
    base_key = jax.random.fold_in(jax.random.fold_in(key, 11), 0)
    block_pos = jnp.arange(NBLK, dtype=jnp.float32) / max(NBLK - 1, 1)
    base_draw = jnp.clip(jax.random.normal(base_key, full_shape, jnp.float32), -4.0, 4.0)
    block_scale = jnp.exp(math.log(3.0) * (block_pos - 1.0))
    leading = NPANEL * PANEL
    column_ids = jnp.arange(W, dtype=jnp.int32)
    shifted = jnp.concatenate([jnp.zeros((NBLK, BLOCK, 1), jnp.float32), base_draw[:, :, :-1]], axis=2)
    mixing = 0.5 * ((column_ids >= 1) & (column_ids < leading)).astype(jnp.float32)
    mixed_cols = (base_draw + mixing[None, None, :] * shifted) * block_scale[:, None, None] * spread
    return jnp.clip(mixed_cols, -8.0 * spread, 8.0 * spread)


def split_up(number_of, total, most, slope):
    portions = [(1 << 20) // math.isqrt(rank ** slope) + 1 for rank in range(2, number_of + 1)]
    surplus, counts = total - most - (number_of - 1), [1] * (number_of - 1)
    while surplus > 0:
        movable = [i for i in range(number_of - 1) if counts[i] < most]
        pool, remaining = sum([portions[i] for i in movable]), surplus
        for i in movable:
            more = min(most - counts[i], max(1, remaining * portions[i] // pool), surplus)
            counts[i] = counts[i] + more
            surplus = surplus - more
    return np.array([most] + counts)


def uneven(own_key, number_of, total, reach, slope):
    if number_of == 2:
        one = jax.random.randint(own_key, (), max(1, total - reach), min(reach, total - 1) + 1)
        return jnp.stack([one, total - one])
    tallies = jnp.asarray(split_up(number_of, total, reach, slope), jnp.int32)
    couples = (number_of - 1) // 2
    giver, sink = tallies[1:1 + 2 * couples:2], tallies[2:2 + 2 * couples:2]
    slack = jnp.minimum(giver - 1, reach - sink)
    moved = jax.random.randint(jax.random.fold_in(own_key, 1), (couples,), 0, 1 << 20) % (slack + 1)
    tallies = tallies.at[1:1 + 2 * couples:2].set(giver - moved).at[2:2 + 2 * couples:2].set(sink + moved)
    return tallies[jax.random.permutation(jax.random.fold_in(own_key, 2), number_of)]


def setup_inputs(seed: int = 0, part: int = 0) -> dict:
    key_of = jax.random.split(jax.random.key(seed), 3)
    part_keys = jax.random.split(jax.random.fold_in(key_of[2], part), 3)
    return {
        "contributions": draw_contributions(jax.random.fold_in(jax.random.fold_in(key_of[2], part), 71), part),
        "valid_rows": uneven(part_keys[1], NBLK, NBLK * 80, BLOCK, 2).astype(jnp.int32),
    }


def reference(contributions, valid_rows):
    blocks, height, width = contributions.shape
    live_rows = (jnp.arange(height, dtype=jnp.int32)[None, :] < valid_rows[:, None]).astype(jnp.float32)
    frontal = (contributions * live_rows[:, :, None]).reshape(blocks * height, width)
    leading = NPANEL * PANEL
    basis, triangle = jnp.linalg.qr(frontal[:, :leading])
    sign_fix = jnp.sign(jnp.diagonal(triangle))
    projected = jnp.dot(basis.T, frontal, precision=lax.Precision.HIGHEST) * sign_fix[:, None]
    kept_mask = jnp.arange(width, dtype=jnp.int32)[None, :] >= jnp.arange(leading, dtype=jnp.int32)[:, None]
    return jnp.where(kept_mask, projected, jnp.zeros_like(projected))
```

```python
import functools

import jax
import jax.numpy as jnp
from jax import lax
from jax.experimental import pallas as pl
from jax.experimental.pallas import tpu as pltpu
from jax.sharding import PartitionSpec as P

PANEL = 256
NPANEL = 2
LANES = 128
SUB = 8
PLANE = 4
HIGHEST = lax.Precision.HIGHEST
MESH = pl.DeviceIdType.MESH


def spread(block, axis, owner):
    block = jnp.where(lax.axis_index(axis) == owner, block, jnp.zeros_like(block))
    return lax.psum(block, axis)


def inner_cols(left, right):
    return jnp.einsum("rp,rc->pc", left, right, precision=HIGHEST)


def by_psum(frontal, leading):
    width_local = frontal.shape[1]
    leading_cols = spread(frontal[:, :leading], "col", 0)
    gram_total = lax.psum(inner_cols(leading_cols, leading_cols), "row")
    factor = jnp.linalg.cholesky(gram_total)
    identity = jnp.eye(leading, dtype=jnp.float32)
    inverse = jax.scipy.linalg.solve_triangular(factor, identity, lower=True)
    first_basis = jnp.dot(leading_cols, inverse.T, precision=HIGHEST)
    projected = lax.psum(inner_cols(first_basis, frontal), "row")
    column_ids = lax.axis_index("col") * width_local + jnp.arange(width_local, dtype=jnp.int32)
    kept_mask = column_ids[None, :] >= jnp.arange(leading, dtype=jnp.int32)[:, None]
    return jnp.where(kept_mask, projected, jnp.zeros_like(projected))


def dot_t(left, right):
    return lax.dot_general(
        left, right, (((0,), (0,)), ((), ())), precision=HIGHEST, preferred_element_type=jnp.float32
    )


def inverse_factor(read, hooks):
    groups = LANES // SUB
    tile = (SUB, LANES)
    row = lax.broadcasted_iota(jnp.int32, tile, 0)
    col = lax.broadcasted_iota(jnp.int32, tile, 1)
    a = [read(g) for g in range(groups)]
    b = [jnp.where(row + g * SUB == col, 1.0, 0.0).astype(jnp.float32) for g in range(groups)]

    def columns(value, home):
        first = home * SUB
        return [jnp.broadcast_to(value[:, first + t : first + t + 1], tile) for t in range(SUB)]

    def across(value, t):
        return jnp.broadcast_to(value[t : t + 1, :], tile)

    for home in range(groups):
        if home in hooks:
            hooks[home]()
        f = columns(a[home], home)
        arow, brow = a[home], b[home]
        scaled, factors = [], []
        diag = f[0]
        for t in range(SUB):
            pinv = 1.0 / across(f[t], t)
            diag = jnp.where(row == t, f[t], diag)
            srow = across(arow, t) * pinv
            trow = across(brow, t) * pinv
            later = [across(f[u], t) * pinv for u in range(t + 1, SUB)]
            below = jnp.where(row > t, f[t], 0.0)
            for u in range(t + 1, SUB):
                f[u] = f[u] - below * later[u - t - 1]
            if t < SUB - 1:
                arow = arow - below * srow
                brow = brow - below * trow
            scaled.append((srow, trow))
            factors.append(later)
        b[home] = brow * lax.rsqrt(diag)
        for g in range(home + 1, groups):
            f = columns(a[g], home)
            for t in range(SUB):
                for u in range(t + 1, SUB):
                    f[u] = f[u] - f[t] * factors[t][u - t - 1]
                a[g] = a[g] - f[t] * scaled[t][0]
                b[g] = b[g] - f[t] * scaled[t][1]
    return b


def kernel(n, leading, f_ref, out_ref, a_pl, f_pl, gram, gram_in, gram_out, part, part_in, gc, inv,
           own_sem, pair_send, pair_recv, ag_send, ag_recv, core_send, core_recv, f_send, f_recv,
           gz_send, gz_recv, gp_send, gp_recv, p_send, p_recv, r_send, r_recv):
    height, width = f_ref.shape
    share = width // n
    half = height // 2
    chunks = leading // LANES
    planes = n // PLANE
    span = planes * share
    slab = LANES // (2 * PLANE)
    stages = n.bit_length() - 1
    r = lax.axis_index("row")
    c = lax.axis_index("col")
    q = lax.rem(r, PLANE)
    z = r // PLANE
    mine = (2 * q + c) * slab
    deltas = [(1 << s) * (1 - 2 * lax.rem(r // (1 << s), 2)) for s in range(stages)]

    def beside(d):
        place = r
        for s in range(stages):
            if (d >> s) & 1:
                place = place + deltas[s]
        return place

    def column(place):
        return pl.multiple_of((lax.rem(place, PLANE) * planes + place // PLANE) * share, share)

    in_plane = list(range(1, PLANE))
    in_line = [PLANE * d for d in range(1, planes)]

    gc[...] = jnp.zeros_like(gc)
    barrier = pltpu.get_barrier_semaphore()
    for d in in_plane + in_line:
        pl.semaphore_signal(barrier, inc=1, device_id={"row": beside(d)}, device_id_type=MESH)
    pl.semaphore_signal(barrier, inc=1, device_id={"col": 1 - c}, device_id_type=MESH)
    pl.semaphore_wait(barrier, len(in_plane) + len(in_line) + 1)

    def to(place):
        return {"device_id": {"row": place}, "device_id_type": MESH}

    other = {"device_id": {"col": 1 - c}, "device_id_type": MESH}
    lead_cols = pl.ds(0, leading)
    lead_steps = [deltas[0] * (1 - c) + deltas[1] * c, deltas[1] * (1 - c) + deltas[0] * c]

    def to_pair(h):
        rows = pl.ds(h * half, half)
        return pltpu.make_async_remote_copy(
            src_ref=f_ref.at[rows, lead_cols], dst_ref=a_pl.at[rows, :],
            send_sem=pair_send.at[h], recv_sem=pair_recv.at[h], **other,
        )

    def lead_half(j):
        slot = (j & 1) * (1 + c) + (j >> 1) * (2 - c)
        return a_pl.at[pl.ds(pl.multiple_of(slot * height + c * half, half), half), :]

    def lead_copy(j, s, src=None):
        k = j + (1 << s)
        return pltpu.make_async_remote_copy(
            src_ref=lead_half(j) if src is None else src, dst_ref=lead_half(k),
            send_sem=ag_send.at[k], recv_sem=ag_recv.at[k], **to(r + lead_steps[s]),
        )

    def core_copy(j):
        return pltpu.make_async_remote_copy(
            src_ref=lead_half(j), dst_ref=lead_half(j),
            send_sem=core_send.at[j], recv_sem=core_recv.at[j], **other,
        )

    own_lead = pltpu.make_async_copy(f_ref.at[:, lead_cols], a_pl.at[pl.ds(0, height), :], own_sem.at[0])
    own_f = pltpu.make_async_copy(
        f_ref.at[:, pl.ds(pl.multiple_of(q * span, span), span)], f_pl.at[pl.ds(0, height), :], own_sem.at[1]
    )

    def f_copy(d):
        place = beside(d)
        return pltpu.make_async_remote_copy(
            src_ref=f_ref.at[:, pl.ds(pl.multiple_of(lax.rem(place, PLANE) * span, span), span)],
            dst_ref=f_pl.at[pl.ds(d * height, height), :],
            send_sem=f_send.at[d], recv_sem=f_recv.at[d], **to(place),
        )

    def tail(k):
        return pl.ds(k * LANES, leading - k * LANES)

    def slab_of(k):
        return pl.ds(pl.multiple_of(k * LANES + mine, slab), slab)

    def gram_line(k, d):
        return pltpu.make_async_remote_copy(
            src_ref=gram.at[slab_of(k), tail(k)], dst_ref=gram_in.at[z, pl.ds(k * slab, slab), tail(k)],
            send_sem=gz_send.at[k, d // PLANE], recv_sem=gz_recv.at[k, d // PLANE], **to(beside(d)),
        )

    def gram_plane(k, i):
        return pltpu.make_async_remote_copy(
            src_ref=gram_out.at[pl.ds(k * slab, slab), tail(k)], dst_ref=gc.at[slab_of(k), tail(k)],
            send_sem=gp_send.at[k, i], recv_sem=gp_recv.at[k, i],
            device_id={"row": beside(i // 2), "col": c + (i % 2) * (1 - 2 * c)}, device_id_type=MESH,
        )

    others = range(1, 2 * PLANE)

    def gram_sum(k):
        for d in in_line:
            gram_line(k, d).wait_recv()
        rows = pl.ds(k * slab, slab)
        gram_in[z, rows, tail(k)] = gram[slab_of(k), tail(k)]
        total = gram_in[0, rows, tail(k)]
        for p in range(1, planes):
            total = total + gram_in[p, rows, tail(k)]
        gram_out[rows, tail(k)] = total
        gc[slab_of(k), tail(k)] = total
        for i in others:
            gram_plane(k, i).start()

    def chunk_rows(k):
        return pl.ds(pl.multiple_of(k * LANES, LANES), LANES)

    def part_copy(k, d):
        place = beside(d)
        return pltpu.make_async_remote_copy(
            src_ref=part.at[chunk_rows(k), pl.ds(pl.multiple_of(place // PLANE * share, share), share)],
            dst_ref=part_in.at[d // PLANE - 1, chunk_rows(k), :],
            send_sem=p_send.at[k, d // PLANE], recv_sem=p_recv.at[k, d // PLANE], **to(place),
        )

    def product(k):
        part[chunk_rows(k), :] = dot_t(a_pl[:, chunk_rows(k)], f_pl[...])
        for d in in_line:
            part_copy(k, d).start()

    def add_product(k):
        for d in in_line:
            part_copy(k, d).wait_recv()
        rows = chunk_rows(k)
        total = part[rows, pl.ds(pl.multiple_of(z * share, share), share)]
        for i in range(planes - 1):
            total = total + part_in[i, rows, :]
        gc[rows, pl.ds(leading, share)] += total

    @pl.when(c == 0)
    def _():
        to_pair(1).start()
        for s in range(2):
            lead_copy(0, s, f_ref.at[pl.ds(0, half), lead_cols]).start()
        to_pair(0).start()
        own_lead.start()

    @pl.when(c == 1)
    def _():
        to_pair(1).wait_recv()
        for s in range(2):
            lead_copy(0, s).start()

    own_f.start()
    lead_copy(0, 0).wait_recv()
    lead_copy(1, 1).start()
    core_copy(1).start()
    lead_copy(0, 1).wait_recv()
    core_copy(2).start()
    for d in reversed(in_plane):
        f_copy(d).start()
    lead_copy(1, 1).wait_recv()
    core_copy(3).start()

    @pl.when(c == 0)
    def _():
        own_lead.wait()

    @pl.when(c == 1)
    def _():
        to_pair(0).wait_recv()

    for j in in_plane:
        core_copy(j).wait_recv()
    for k in range(chunks):
        rows = pl.ds(k * LANES, LANES)
        gram[rows, tail(k)] = dot_t(a_pl[:, rows], a_pl[:, tail(k)])
        for d in in_line:
            gram_line(k, d).start()
    gram_sum(0)
    own_f.wait()
    for d in in_plane:
        f_copy(d).wait_recv()
    product(0)
    for k in range(1, chunks):
        gram_sum(k)
    product(1)
    for i in others:
        gram_plane(0, i).wait_recv()

    def steps_of(parity):
        return [
            deltas[3], deltas[2],
            deltas[1] * (1 - parity) + deltas[0] * parity,
            deltas[0] * (1 - parity) + deltas[1] * parity,
        ]

    def out_piece(k, j, steps):
        place = r
        for s in range(stages):
            if (j >> s) & 1:
                place = place + steps[s]
        return out_ref.at[chunk_rows(k), pl.ds(column(place), share)]

    def out_copy(k, j, s):
        steps = steps_of(lax.rem(k + c, 2))
        return pltpu.make_async_remote_copy(
            src_ref=out_piece(k, j, steps), dst_ref=out_piece(k, j, steps),
            send_sem=r_send.at[k, j + (1 << s)], recv_sem=r_recv.at[k, j + (1 << s)], **to(r + steps[s]),
        )

    def forward(k, top):
        for j in range(1 << top, 2 << top):
            out_copy(k, j - (1 << top), top).wait_recv()
            for s in range(top + 1, stages):
                out_copy(k, j, s).start()

    first_col = c * width + column(r)
    row_id = lax.broadcasted_iota(jnp.int32, (LANES, share), 0)
    col_id = lax.broadcasted_iota(jnp.int32, (LANES, share), 1) + first_col

    @pl.loop(0, chunks)
    def _(k):
        base = pl.multiple_of(k * LANES, LANES)
        ks = pl.ds(base, LANES)

        def read(g):
            return gc[pl.ds(pl.multiple_of(base + g * SUB, SUB), SUB), ks]

        def hook(back, top):
            def run():
                @pl.when(k >= back)
                def _():
                    forward(k - back, top)
            return run

        groups = LANES // SUB
        hooks = {2: hook(2, stages - 2)}
        for s in range(stages - 2):
            hooks[groups * (s + 1) // (stages - 1) + 1] = hook(1, s)
        b = inverse_factor(read, hooks)
        for g, rows in enumerate(b):
            inv[pl.ds(g * SUB, SUB), :] = rows
        add_product(k)
        rows = jnp.dot(inv[...], gc[ks, :], precision=HIGHEST, preferred_element_type=jnp.float32)
        out_ref[ks, pl.ds(column(r), share)] = jnp.where(col_id >= row_id + base, rows[:, leading:], 0.0)
        for s in range(stages):
            out_copy(k, 0, s).start()
        gc[ks, :] = rows

        @pl.when(k == 0)
        def _():
            for g in range(1, chunks):
                for i in others:
                    gram_plane(g, i).wait_recv()

        for i in range(1, chunks):
            @pl.when(i > k)
            def _():
                left = gc[ks, pl.ds(i * LANES, LANES)]
                rest = pl.ds(i * LANES, leading + share - i * LANES)
                gc[pl.ds(i * LANES, LANES), rest] -= dot_t(left, gc[ks, rest])

        @pl.when(k + 2 < chunks)
        def _():
            product(k + 2)

    forward(chunks - 2, stages - 2)
    for top in range(stages - 1):
        forward(chunks - 1, top)
    for k in range(chunks):
        forward(k, stages - 1)

    @pl.when(c == 0)
    def _():
        for h in range(2):
            to_pair(h).wait_send()

    for d in in_plane:
        lead_copy(0 if d < 3 else 1, 0 if d == 1 else 1).wait_send()
        core_copy(d).wait_send()
        f_copy(d).wait_send()
    for k in range(chunks):
        for d in in_line:
            gram_line(k, d).wait_send()
            part_copy(k, d).wait_send()
        for i in others:
            gram_plane(k, i).wait_send()
        for j in range(1, n):
            top = j.bit_length() - 1
            out_copy(k, j - (1 << top), top).wait_send()


def by_kernel(frontal, leading, n):
    height, width = frontal.shape
    share = width // n
    chunks = leading // LANES
    planes = n // PLANE
    slab = LANES // (2 * PLANE)
    dma = pltpu.SemaphoreType.DMA
    return pl.pallas_call(
        functools.partial(kernel, n, leading),
        out_shape=jax.ShapeDtypeStruct((leading, width), jnp.float32),
        in_specs=[pl.BlockSpec(memory_space=pltpu.VMEM)],
        out_specs=pl.BlockSpec(memory_space=pltpu.VMEM),
        scratch_shapes=[
            pltpu.VMEM((PLANE * height, leading), jnp.float32),
            pltpu.VMEM((PLANE * height, planes * share), jnp.float32),
            pltpu.VMEM((leading, leading), jnp.float32),
            pltpu.VMEM((planes, chunks * slab, leading), jnp.float32),
            pltpu.VMEM((chunks * slab, leading), jnp.float32),
            pltpu.VMEM((leading, planes * share), jnp.float32),
            pltpu.VMEM((planes - 1, leading, share), jnp.float32),
            pltpu.VMEM((leading, leading + share), jnp.float32),
            pltpu.VMEM((LANES, LANES), jnp.float32),
            dma((2,)), dma((2,)), dma((2,)), dma((PLANE,)), dma((PLANE,)), dma((PLANE,)), dma((PLANE,)),
            dma((PLANE,)), dma((PLANE,)),
            dma((chunks, planes)), dma((chunks, planes)),
            dma((chunks, 2 * PLANE)), dma((chunks, 2 * PLANE)),
            dma((chunks, planes)), dma((chunks, planes)),
            dma((chunks, n)), dma((chunks, n)),
        ],
        compiler_params=pltpu.CompilerParams(
            collective_id=0, has_side_effects=True, vmem_limit_bytes=48 << 20
        ),
        name="front_rows",
    )(frontal)


def body(n, pair, contributions, valid_rows):
    blocks, height, width_local = contributions.shape
    live_rows = jnp.arange(height, dtype=jnp.int32)[None, :] < valid_rows[:, None]
    frontal = jnp.where(live_rows[:, :, None], contributions, 0.0).reshape(blocks * height, width_local)
    leading = NPANEL * PANEL
    rows = blocks * height
    fits = (
        pair == 2 and n == PLANE * PLANE and width_local == n * LANES
        and rows == LANES and leading % LANES == 0 and leading <= width_local
    )
    if fits:
        return by_kernel(frontal, leading, n)
    return by_psum(frontal, leading)


def solution(mesh):
    return jax.shard_map(
        functools.partial(body, mesh.shape["row"], mesh.shape["col"]),
        mesh=mesh,
        in_specs=(P(("front", "row"), None, "col"), P(("front", "row"))),
        out_specs=P("front", "col"),
        check_vma=False,
    )
```
